256 devices in a mesh: chan: 8 (over z_lo, y), win: 32 (over x, z_hi, core).
Axes of the slice: x: 4, y: 4, z: 8 (z_hi: 4, z_lo: 2; z = z_hi * 2 + z_lo), core: 2. Of those that a mesh axis runs over, the one named last changes fastest.
Arguments:
- raw_traces: bfloat16 [32, 2048, 512], P('win', 'chan'), may hold values from -6 to 6
- fir_taps: float32 [65], replicated, may hold values from -0.75 to 0.75
- source_blocks: int32 [2], replicated, may hold values from 0 to 31
- valid_counts: int32 [32, 2048], P('win', 'chan'), may hold values from 0 to 512, as said below
Outputs:
- stack: float32 [128, 201, 2048], P('win', None, 'chan')
The draws below stay inside these ranges and needn't reach their ends.
Inputs may be any that keep to these rules, and one draw needn't show every extreme that they name: `valid_counts`: 0 marks a dead channel, and every window has one.
All inputs are finite; a program needn't handle non-finite values.
Results may differ from the reference program's by a relative error of at most 0.0028.
Values may be sent and summed in bfloat16 or wider, within the bound.
No kernel may reach another device: no remote copies, remote signals or barrier semaphores. Data moves between devices by JAX's collectives and lax.ppermute only.
A program may use at most 192 MiB of HBM per device.

```python
import math
import jax
import jax.numpy as jnp
from jax import lax

C = 2048
BLK = 64
NBLK = 2
SAMP = 512
TAPS = 65
HALFRUN = 64
MAXLAG = 100
NWIN = 32


def draw_valid_counts(key, part):
    key_kind, key_part, key_dead = jax.random.split(key, 3)
    kinds = jax.random.randint(key_kind, (NWIN, C), 0, 8)
    partial_counts = jax.random.randint(key_part, (NWIN, C), 1, SAMP)
    dead_column = jax.random.randint(key_dead, (NWIN, 1), 0, C)
    columns = jnp.arange(C, dtype=jnp.int32)[None, :]
    counts = jnp.where(kinds == 0, 0, jnp.where(kinds <= 2, partial_counts, SAMP))
    return jnp.where(columns == dead_column, 0, counts).astype(jnp.int32)


def shard_levels(key, extent, cuts, smallest, top_value):
    factor_of = 1.0
    for axis_at, blocks in cuts:
        draws = jax.random.uniform(jax.random.fold_in(jax.random.fold_in(key, 6), axis_at), (blocks,), jnp.float32, smallest / len(cuts), top_value / len(cuts))
        factor_of = factor_of * jnp.repeat(jnp.exp(draws), extent[axis_at] // blocks).reshape((-1,) + (1,) * (len(extent) - 1 - axis_at))
    return factor_of


def scatter_about(own_key, shape, width, limit, pieces=(), held_as=jnp.bfloat16):
    loudness = shard_levels(own_key, shape, pieces, -0.22, 0.18) if pieces else 1.0
    values = jax.random.normal(own_key, shape, jnp.float32) * width * loudness
    return jnp.minimum(jnp.maximum(values, -limit), limit).astype(held_as)


def setup_inputs(seed: int = 0) -> dict:
    keys = jax.random.split(jax.random.key(seed), 5)
    return {
        "raw_traces": scatter_about(keys[0], (NWIN, C, SAMP), 1.0, 6.0, ((0, 32), (1, 8))),
        "fir_taps": scatter_about(keys[1], (TAPS,), TAPS ** -0.5, 0.75, (), jnp.float32),
        "source_blocks": jax.random.randint(keys[2], (NBLK,), 0, C // BLK).astype(jnp.int32),
        "valid_counts": draw_valid_counts(jax.random.fold_in(keys[4], 71), 0),
    }


def prepare(raw_traces, fir_taps, valid_counts):
    samples = raw_traces.shape[-1]
    flattened = raw_traces.astype(jnp.float32).reshape(-1, 1, samples)
    kernel = fir_taps.astype(jnp.float32).reshape(1, 1, -1)
    half_taps = (fir_taps.shape[0] - 1) // 2
    filtered = lax.conv_general_dilated(flattened, kernel, (1,), [(half_taps, half_taps)], precision=lax.Precision.HIGHEST).reshape(raw_traces.shape)
    positions = jnp.arange(samples, dtype=jnp.int32)
    banded = (jnp.abs(positions[:, None] - positions[None, :]) <= HALFRUN).astype(jnp.float32)
    counted = lax.optimization_barrier(jnp.sum(banded, axis=0))
    envelope = jnp.dot(jnp.abs(filtered).reshape(-1, samples), banded, precision=lax.Precision.HIGHEST).reshape(filtered.shape) / counted
    whitened = filtered / (envelope + 1e-06)
    is_live = positions < valid_counts[..., None]
    return jnp.where(is_live, whitened, 0.0).astype(jnp.bfloat16)

def lagged_rows(row_data):
    samples = row_data.shape[-1]
    padding = [(0, 0)] * (row_data.ndim - 1) + [(MAXLAG, MAXLAG)]
    padded = jnp.pad(row_data, padding)
    return jnp.stack([padded[..., 2 * MAXLAG - offset:2 * MAXLAG - offset + samples] for offset in range(2 * MAXLAG + 1)], axis=-2)

def reference(raw_traces, fir_taps, source_blocks, valid_counts):
    whitened = lax.map(lambda paired: prepare(paired[0], fir_taps, paired[1]), (raw_traces, valid_counts))
    sources = jnp.concatenate([lax.dynamic_slice_in_dim(whitened, (source_blocks[number] * BLK).astype(jnp.int32), BLK, 1) for number in range(NBLK)], axis=1)

    def per_window(summed, paired):
        source_rows, receivers = paired
        lagged = lagged_rows(source_rows).astype(jnp.float32)
        return (summed + jnp.einsum('slu,ru->slr', lagged, receivers.astype(jnp.float32)), None)
    zeroed = jnp.zeros((sources.shape[1], 2 * MAXLAG + 1, whitened.shape[1]), jnp.float32)
    summed, _ = lax.scan(per_window, zeroed, (sources, whitened))
    return summed / math.sqrt(SAMP * whitened.shape[0])
```

```python
import math

import jax
import jax.numpy as jnp
from jax import lax
from jax.experimental import pallas as pl
from jax.experimental.pallas import tpu as pltpu
from jax.sharding import Mesh, PartitionSpec as P

BLK = 64
NBLK = 2
SAMP = 512
TAPS = 65
HALFTAPS = 32
HALFRUN = 64
MAXLAG = 100
NLAG = 2 * MAXLAG + 1
LAGPAD = 208
SRC_PAIR = 8
CHUNKS = ((0, 256), (256, 256))


def split_terms(x):
    hi = x.astype(jnp.bfloat16)
    rest = x - hi.astype(jnp.float32)
    mid = rest.astype(jnp.bfloat16)
    lo = (rest - mid.astype(jnp.float32)).astype(jnp.bfloat16)
    return hi, mid, lo


def dot_t(a, b):
    return lax.dot_general(a, b, (((1,), (1,)), ((), ())), preferred_element_type=jnp.float32)


def prep_body(blocks_ref, chan_ref, raw_ref, taps_ref, counts_ref, *refs):
    out_refs, contrib_ref, full_ref = refs[:-2], refs[-2], refs[-1]
    channels = raw_ref.shape[0]
    side = jnp.zeros((channels, 128), jnp.bfloat16)
    raw = jnp.concatenate([side, raw_ref[...], side], axis=1)
    rows = jnp.broadcast_to(taps_ref[...], (256, 512))
    strips = split_terms(pltpu.roll(rows, 0, 1, stride=1, stride_axis=0))
    filtered = []
    for m in range(2):
        part = raw[:, 256 * m : 256 * m + 512]
        filtered.append(dot_t(part, strips[0]) + (dot_t(part, strips[1]) + dot_t(part, strips[2])))
    filtered = jnp.concatenate(filtered, axis=1)
    at_row = lax.broadcasted_iota(jnp.int32, (256, 512), 0) + 128
    at_col = lax.broadcasted_iota(jnp.int32, (256, 512), 1)
    band = jnp.where(jnp.abs(at_row - at_col) <= HALFRUN, 1.0, 0.0).astype(jnp.bfloat16)
    pieces = [jnp.concatenate([side, t, side], axis=1) for t in split_terms(jnp.abs(filtered))]
    summed = []
    for m in range(2):
        cut = [p[:, 256 * m : 256 * m + 512] for p in pieces]
        summed.append(dot_t(cut[0], band) + (dot_t(cut[1], band) + dot_t(cut[2], band)))
    summed = jnp.concatenate(summed, axis=1)
    at = lax.broadcasted_iota(jnp.int32, (1, SAMP), 1)
    counted = jnp.minimum(at + HALFRUN, SAMP - 1) - jnp.maximum(at - HALFRUN, 0) + 1
    envelope = summed / counted.astype(jnp.float32)
    whitened = filtered / (envelope + 1e-06)
    counts = jnp.broadcast_to(counts_ref[...].astype(jnp.float32), (128, channels)).T
    counts = jnp.concatenate([counts] * (SAMP // 128), axis=1)
    live = at.astype(jnp.float32) < counts
    whitened = jnp.where(live, whitened, 0.0)
    rounded = whitened.astype(jnp.bfloat16)
    for ref, (start, width) in zip(out_refs, CHUNKS):
        ref[...] = rounded[:, start : start + width]
    full_ref[...] = rounded
    held = channels // BLK
    for number in range(NBLK):
        local = blocks_ref[number] - chan_ref[0] * held
        owned = jnp.logical_and(local >= 0, local < held)
        start = pl.multiple_of(jnp.clip(local, 0, held - 1) * BLK, BLK)
        rows = full_ref[pl.ds(start, BLK), :].astype(jnp.float32)
        rows = jnp.where(owned, rows, 0.0)
        contrib_ref[number * BLK : (number + 1) * BLK, :] = rows.astype(jnp.bfloat16)


def prep(raw, fir_taps, source_blocks, counts, chan):
    channels = raw.shape[0]
    taps = jnp.pad(fir_taps.reshape(1, TAPS), ((0, 0), (128 - HALFTAPS, 512 - TAPS - 128 + HALFTAPS)))
    smem = pl.BlockSpec(memory_space=pltpu.SMEM)
    vmem = pl.BlockSpec(memory_space=pltpu.VMEM)
    return pl.pallas_call(
        prep_body,
        in_specs=[smem, smem, vmem, vmem, vmem],
        out_specs=[vmem] * (len(CHUNKS) + 1),
        out_shape=[jax.ShapeDtypeStruct((channels, width), jnp.bfloat16) for _, width in CHUNKS]
        + [jax.ShapeDtypeStruct((NBLK * BLK, SAMP), jnp.bfloat16)],
        scratch_shapes=[pltpu.VMEM((channels, SAMP), jnp.bfloat16)],
        name="prep",
    )(source_blocks, chan, raw, taps, counts)


def fill_lagged(rows, first, lagged_ref, start, width):
    low, high = start - 256, start + width + 128
    parts = []
    if low < 0:
        parts.append(jnp.zeros((SRC_PAIR, -low), jnp.float32))
    parts.append(rows[:, max(low, 0) : min(high, SAMP)])
    if high > SAMP:
        parts.append(jnp.zeros((SRC_PAIR, high - SAMP), jnp.float32))
    around = jnp.concatenate(parts, axis=1) if len(parts) > 1 else parts[0]
    span = high - low
    shift = 128 - MAXLAG - 256
    around = pltpu.roll(around, shift % 8, 1)
    shift = (shift - shift % 8) % span
    for at in range(SRC_PAIR // 2):
        row = jnp.broadcast_to(around[first + at : first + at + 1, :], (128, span))
        rolled = pltpu.roll(row, shift, 1, stride=1, stride_axis=0).astype(jnp.bfloat16)
        lagged_ref[at * LAGPAD : at * LAGPAD + 128, :] = rolled[:, 128 : 128 + width]
        lagged_ref[at * LAGPAD + 128 : (at + 1) * LAGPAD, :] = rolled[: LAGPAD - 128, :width]


def correlate_body(start, width, has_prev, is_last, *refs):
    refs = list(refs)
    core_ref = refs.pop(0) if is_last else None
    src_ref, recv_ref = refs.pop(0), refs.pop(0)
    prev_ref = refs.pop(0) if has_prev else None
    if is_last:
        mine_ref, other_ref, acc_ref, first_ref, second_ref = refs
    else:
        acc_ref, first_ref, second_ref = refs
    window = pl.program_id(0)

    @pl.when(window == 0)
    def _():
        acc_ref[...] = prev_ref[...] if has_prev else jnp.zeros(acc_ref.shape, jnp.float32)

    rows = src_ref[0].astype(jnp.float32)
    receivers = recv_ref[0]
    half = SRC_PAIR // 2
    for number, lagged_ref in enumerate((first_ref, second_ref)):
        fill_lagged(rows, number * half, lagged_ref, start, width)
        got = dot_t(lagged_ref[...], receivers).reshape(half, LAGPAD, receivers.shape[0])
        acc_ref[number * half : (number + 1) * half] += got

    if is_last:

        @pl.when(window == pl.num_programs(0) - 1)
        def _():
            core = core_ref[0]
            mine_ref[...] = acc_ref[pl.ds(core * half, half), :NLAG, :]
            other_ref[...] = acc_ref[pl.ds((1 - core) * half, half), :NLAG, :]


def correlate(sources, receivers, prev, core, number):
    start, width = CHUNKS[number]
    is_last = number == len(CHUNKS) - 1
    windows, local_width = receivers.shape[0], receivers.shape[1]
    acc_shape = (SRC_PAIR, LAGPAD, local_width)
    whole = lambda shape: pl.BlockSpec(shape, lambda w: (0,) * len(shape))
    half_shape = (SRC_PAIR // 2, NLAG, local_width)
    in_specs = [
        pl.BlockSpec((1, SRC_PAIR, SAMP), lambda w: (w, 0, 0)),
        pl.BlockSpec((1, local_width, width), lambda w: (w, 0, 0)),
    ]
    operands = [sources, receivers]
    if is_last:
        in_specs.insert(0, pl.BlockSpec(memory_space=pltpu.SMEM))
        operands.insert(0, core)
    if prev is not None:
        in_specs.append(whole(acc_shape))
        operands.append(prev)
    scratch = [pltpu.VMEM((SRC_PAIR // 2 * LAGPAD, width), jnp.bfloat16)] * 2
    if is_last:
        out_specs = [whole(half_shape)] * 2
        out_shape = [jax.ShapeDtypeStruct(half_shape, jnp.float32)] * 2
        scratch = [pltpu.VMEM(acc_shape, jnp.float32)] + scratch
    else:
        out_specs = whole(acc_shape)
        out_shape = jax.ShapeDtypeStruct(acc_shape, jnp.float32)

    def body(*refs):
        correlate_body(start, width, prev is not None, is_last, *refs)

    return pl.pallas_call(
        body,
        grid=(windows,),
        in_specs=in_specs,
        out_specs=out_specs,
        out_shape=out_shape,
        scratch_shapes=scratch,
        name=f"correlate_{number}",
    )(*operands)


def shards(raw_traces, fir_taps, source_blocks, valid_counts):
    chan = lax.axis_index("chan").astype(jnp.int32)
    core = lax.axis_index("core").astype(jnp.int32).reshape(1)
    chans = lax.axis_size("chan")
    spread = lax.axis_size("spread")
    *chunks, mine = prep(raw_traces[0], fir_taps, source_blocks, valid_counts, chan.reshape(1))
    gathered = [lax.all_gather(c, "spread", axis=0) for c in chunks]
    step = 1
    while step < chans:
        mine = mine + lax.ppermute(mine, "chan", [(i, i ^ step) for i in range(chans)])
        step *= 2
    mine = mine.reshape(spread, SRC_PAIR, SAMP)
    sources = lax.all_to_all(mine, "spread", split_axis=0, concat_axis=0, tiled=True)
    total = None
    for number, receivers in enumerate(gathered):
        total = correlate(sources, receivers, total, core, number)
    kept, passed = total
    got = lax.ppermute(passed, "core", [(0, 1), (1, 0)])
    factor = 1.0 / math.sqrt(SAMP * raw_traces.shape[0] * spread * 2)
    return (kept + got) * factor


def solution(mesh):
    chans, wins = mesh.devices.shape
    finer = Mesh(mesh.devices.reshape(chans, wins // 2, 2), ("chan", "spread", "core"))
    win = ("spread", "core")
    return jax.shard_map(
        shards,
        mesh=finer,
        in_specs=(P(win, "chan", None), P(), P(), P(win, "chan")),
        out_specs=P(win, None, "chan"),
        check_vma=False,
    )
```

```python
import math

import jax
import jax.numpy as jnp
from jax import lax
from jax.experimental import pallas as pl
from jax.experimental.pallas import tpu as pltpu
from jax.sharding import Mesh, PartitionSpec as P

BLK = 64
NBLK = 2
SAMP = 512
TAPS = 65
HALFTAPS = 32
HALFRUN = 64
MAXLAG = 100
NLAG = 2 * MAXLAG + 1
LAGPAD = 208
SRC_PAIR = 8
CHUNKS = ((0, 512),)


def split_terms(x):
    hi = x.astype(jnp.bfloat16)
    rest = x - hi.astype(jnp.float32)
    mid = rest.astype(jnp.bfloat16)
    lo = (rest - mid.astype(jnp.float32)).astype(jnp.bfloat16)
    return hi, mid, lo


def dot_t(a, b):
    return lax.dot_general(a, b, (((1,), (1,)), ((), ())), preferred_element_type=jnp.float32)


def prep_body(blocks_ref, chan_ref, raw_ref, taps_ref, counts_ref, *refs):
    out_refs, contrib_ref, full_ref = refs[:-2], refs[-2], refs[-1]
    channels = raw_ref.shape[0]
    side = jnp.zeros((channels, 128), jnp.bfloat16)
    raw = jnp.concatenate([side, raw_ref[...], side], axis=1)
    rows = jnp.broadcast_to(taps_ref[...], (256, 512))
    strips = split_terms(pltpu.roll(rows, 0, 1, stride=1, stride_axis=0))
    filtered = []
    for m in range(2):
        part = raw[:, 256 * m : 256 * m + 512]
        filtered.append(dot_t(part, strips[0]) + (dot_t(part, strips[1]) + dot_t(part, strips[2])))
    filtered = jnp.concatenate(filtered, axis=1)
    at_row = lax.broadcasted_iota(jnp.int32, (256, 512), 0) + 128
    at_col = lax.broadcasted_iota(jnp.int32, (256, 512), 1)
    band = jnp.where(jnp.abs(at_row - at_col) <= HALFRUN, 1.0, 0.0).astype(jnp.bfloat16)
    pieces = [jnp.concatenate([side, t, side], axis=1) for t in split_terms(jnp.abs(filtered))]
    summed = []
    for m in range(2):
        cut = [p[:, 256 * m : 256 * m + 512] for p in pieces]
        summed.append(dot_t(cut[0], band) + (dot_t(cut[1], band) + dot_t(cut[2], band)))
    summed = jnp.concatenate(summed, axis=1)
    at = lax.broadcasted_iota(jnp.int32, (1, SAMP), 1)
    counted = jnp.minimum(at + HALFRUN, SAMP - 1) - jnp.maximum(at - HALFRUN, 0) + 1
    envelope = summed / counted.astype(jnp.float32)
    whitened = filtered / (envelope + 1e-06)
    counts = jnp.broadcast_to(counts_ref[...].astype(jnp.float32), (128, channels)).T
    counts = jnp.concatenate([counts] * (SAMP // 128), axis=1)
    live = at.astype(jnp.float32) < counts
    whitened = jnp.where(live, whitened, 0.0)
    rounded = whitened.astype(jnp.bfloat16)
    for ref, (start, width) in zip(out_refs, CHUNKS):
        ref[...] = rounded[:, start : start + width]
    full_ref[...] = rounded
    held = channels // BLK
    for number in range(NBLK):
        local = blocks_ref[number] - chan_ref[0] * held
        owned = jnp.logical_and(local >= 0, local < held)
        start = pl.multiple_of(jnp.clip(local, 0, held - 1) * BLK, BLK)
        rows = full_ref[pl.ds(start, BLK), :].astype(jnp.float32)
        rows = jnp.where(owned, rows, 0.0)
        contrib_ref[number * BLK : (number + 1) * BLK, :] = rows.astype(jnp.bfloat16)


def prep(raw, fir_taps, source_blocks, counts, chan):
    channels = raw.shape[0]
    taps = jnp.pad(fir_taps.reshape(1, TAPS), ((0, 0), (128 - HALFTAPS, 512 - TAPS - 128 + HALFTAPS)))
    smem = pl.BlockSpec(memory_space=pltpu.SMEM)
    vmem = pl.BlockSpec(memory_space=pltpu.VMEM)
    return pl.pallas_call(
        prep_body,
        in_specs=[smem, smem, vmem, vmem, vmem],
        out_specs=[vmem] * (len(CHUNKS) + 1),
        out_shape=[jax.ShapeDtypeStruct((channels, width), jnp.bfloat16) for _, width in CHUNKS]
        + [jax.ShapeDtypeStruct((NBLK * BLK, SAMP), jnp.bfloat16)],
        scratch_shapes=[pltpu.VMEM((channels, SAMP), jnp.bfloat16)],
        name="prep",
    )(source_blocks, chan, raw, taps, counts)


def fill_lagged(rows, first, lagged_ref, start, width):
    low, high = start - 256, start + width + 128
    parts = []
    if low < 0:
        parts.append(jnp.zeros((SRC_PAIR, -low), jnp.float32))
    parts.append(rows[:, max(low, 0) : min(high, SAMP)])
    if high > SAMP:
        parts.append(jnp.zeros((SRC_PAIR, high - SAMP), jnp.float32))
    around = jnp.concatenate(parts, axis=1) if len(parts) > 1 else parts[0]
    span = high - low
    shift = 128 - MAXLAG - 256
    around = pltpu.roll(around, shift % 8, 1)
    shift = (shift - shift % 8) % span
    for at in range(SRC_PAIR // 2):
        row = jnp.broadcast_to(around[first + at : first + at + 1, :], (128, span))
        rolled = pltpu.roll(row, shift, 1, stride=1, stride_axis=0).astype(jnp.bfloat16)
        lagged_ref[at * LAGPAD : at * LAGPAD + 128, :] = rolled[:, 128 : 128 + width]
        lagged_ref[at * LAGPAD + 128 : (at + 1) * LAGPAD, :] = rolled[: LAGPAD - 128, :width]


def correlate_body(start, width, has_prev, is_last, *refs):
    refs = list(refs)
    _, core_ref, src_ref, recv_ref = refs[:4]
    refs = refs[4:]
    prev_ref = refs.pop(0) if has_prev else None
    if is_last:
        mine_ref, other_ref, acc_ref, first_ref, second_ref = refs
    else:
        acc_ref, first_ref, second_ref = refs
    window = pl.program_id(0)

    @pl.when(window == 0)
    def _():
        acc_ref[...] = prev_ref[...] if has_prev else jnp.zeros(acc_ref.shape, jnp.float32)

    rows = src_ref[0].astype(jnp.float32)
    receivers = recv_ref[0]
    half = SRC_PAIR // 2
    for number, lagged_ref in enumerate((first_ref, second_ref)):
        fill_lagged(rows, number * half, lagged_ref, start, width)
        got = dot_t(lagged_ref[...], receivers).reshape(half, LAGPAD, receivers.shape[0])
        acc_ref[number * half : (number + 1) * half] += got

    if is_last:

        @pl.when(window == pl.num_programs(0) - 1)
        def _():
            core = core_ref[0]
            mine_ref[...] = acc_ref[pl.ds(core * half, half), :NLAG, :]
            other_ref[...] = acc_ref[pl.ds((1 - core) * half, half), :NLAG, :]


def correlate(sources, receivers, windows_of, base, prev, core, chunk, is_last):
    start, width = chunk
    windows, local_width = receivers.shape[0], receivers.shape[1]
    acc_shape = (SRC_PAIR, LAGPAD, local_width)
    whole = lambda shape: pl.BlockSpec(shape, lambda w, table, core: (0,) * len(shape))
    half_shape = (SRC_PAIR // 2, NLAG, local_width)
    in_specs = [
        pl.BlockSpec((1, SRC_PAIR, SAMP), lambda w, table, core: (table[base + w], 0, 0)),
        pl.BlockSpec((1, local_width, width), lambda w, table, core: (w, 0, 0)),
    ]
    operands = [sources, receivers]
    if prev is not None:
        in_specs.append(whole(acc_shape))
        operands.append(prev)
    scratch = [pltpu.VMEM((SRC_PAIR // 2 * LAGPAD, width), jnp.bfloat16)] * 2
    if is_last:
        out_specs = [whole(half_shape)] * 2
        out_shape = [jax.ShapeDtypeStruct(half_shape, jnp.float32)] * 2
        scratch = [pltpu.VMEM(acc_shape, jnp.float32)] + scratch
    else:
        out_specs = whole(acc_shape)
        out_shape = jax.ShapeDtypeStruct(acc_shape, jnp.float32)

    def body(*refs):
        correlate_body(start, width, prev is not None, is_last, *refs)

    return pl.pallas_call(
        body,
        grid_spec=pltpu.PrefetchScalarGridSpec(
            num_scalar_prefetch=2,
            grid=(windows,),
            in_specs=in_specs,
            out_specs=out_specs,
            scratch_shapes=scratch,
        ),
        out_shape=out_shape,
        name="correlate",
    )(windows_of, core, *operands)


def ring_offset(step):
    return jnp.where(step == 3, 2, jnp.where(step == 2, 1, -step))


def shifted(value, axis, by):
    size = lax.axis_size(axis)
    return lax.ppermute(value, axis, [(i, (i + by) % size) for i in range(size)])


def along_z(own):
    below, above = shifted(own, "z_hi", 1), shifted(own, "z_hi", -1)
    half = own.shape[0] // 2
    low = shifted(below[:half], "z_hi", 1)
    high = shifted(above[half:], "z_hi", -1)
    return jnp.stack([own, below, above, jnp.concatenate([low, high], axis=0)])


def along_x(bundle, before, after):
    half = bundle.shape[0] // 2
    low = shifted(before[:half], "x", 1)
    high = shifted(after[half:], "x", -1)
    return [bundle, before, after, low, high]


def shards(raw_traces, fir_taps, source_blocks, valid_counts):
    chan = lax.axis_index("chan").astype(jnp.int32)
    core = lax.axis_index("core").astype(jnp.int32).reshape(1)
    at_x = lax.axis_index("x").astype(jnp.int32)
    at_z = lax.axis_index("z_hi").astype(jnp.int32)
    chans, size_x, size_z = lax.axis_size("chan"), lax.axis_size("x"), lax.axis_size("z_hi")
    *chunks, mine = prep(raw_traces[0], fir_taps, source_blocks, valid_counts, chan.reshape(1))
    bundles = [along_z(c) for c in chunks]
    step = 1
    while step < chans:
        mine = mine + lax.ppermute(mine, "chan", [(i, i ^ step) for i in range(chans)])
        step *= 2
    mine, *bundles = lax.optimization_barrier((mine, *bundles))
    mine = mine.reshape(size_x * size_z, SRC_PAIR, SAMP)
    sources = lax.all_to_all(mine, ("x", "z_hi"), split_axis=0, concat_axis=0, tiled=True)
    sent = [(shifted(b, "x", 1), shifted(b, "x", -1)) for b in bundles]
    sources, sent = lax.optimization_barrier((sources, sent))
    bundles = [along_x(b, *pair) for b, pair in zip(bundles, sent)]
    steps = jnp.arange(size_x * size_z, dtype=jnp.int32)
    off_x, off_z = ring_offset(steps >> 2), ring_offset(steps & 3)
    windows_of = ((at_x + off_x) & (size_x - 1)) * size_z + ((at_z + off_z) & (size_z - 1))
    work = [(c, piece) for c, pieces in zip(CHUNKS, bundles) for piece in pieces]
    total, base = None, 0
    for number, (chunk, receivers) in enumerate(work):
        is_last = number == len(work) - 1
        total = correlate(sources, receivers, windows_of, base, total, core, chunk, is_last)
        base = (base + receivers.shape[0]) % (size_x * size_z)
    kept, passed = total
    got = shifted(passed, "core", 1)
    factor = 1.0 / math.sqrt(SAMP * size_x * size_z * 2)
    return (kept + got) * factor


def solution(mesh):
    chans, wins = mesh.devices.shape
    finer = Mesh(
        mesh.devices.reshape(chans, 4, wins // 8, 2), ("chan", "x", "z_hi", "core")
    )
    win = ("x", "z_hi", "core")
    return jax.shard_map(
        shards,
        mesh=finer,
        in_specs=(P(win, "chan", None), P(), P(), P(win, "chan")),
        out_specs=P(win, None, "chan"),
        check_vma=False,
    )
```

```python
import math

import jax
import jax.numpy as jnp
from jax import lax
from jax.experimental import pallas as pl
from jax.experimental.pallas import tpu as pltpu
from jax.sharding import Mesh, PartitionSpec as P

BLK = 64
NBLK = 2
SAMP = 512
TAPS = 65
HALFTAPS = 32
HALFRUN = 64
MAXLAG = 100
NLAG = 2 * MAXLAG + 1
LAGPAD = 208
SRC_PAIR = 8


def split_terms(x):
    hi = x.astype(jnp.bfloat16)
    rest = x - hi.astype(jnp.float32)
    mid = rest.astype(jnp.bfloat16)
    lo = (rest - mid.astype(jnp.float32)).astype(jnp.bfloat16)
    return hi, mid, lo


def dot_t(a, b):
    return lax.dot_general(a, b, (((1,), (1,)), ((), ())), preferred_element_type=jnp.float32)


def prep_body(blocks_ref, chan_ref, raw_ref, taps_ref, counts_ref, *refs):
    out_ref, contrib_ref, padded_ref = refs
    full_ref = out_ref
    channels = raw_ref.shape[0]
    side = jnp.zeros((channels, 128), jnp.bfloat16)
    raw = jnp.concatenate([side, raw_ref[...], side], axis=1)
    padded_ref[...] = jnp.zeros(padded_ref.shape, jnp.float32)
    padded_ref[:, :TAPS] = taps_ref[...]
    rows = jnp.broadcast_to(padded_ref[...], (256, 512))
    strips = split_terms(pltpu.roll(rows, 128 - HALFTAPS, 1, stride=1, stride_axis=0))
    filtered = []
    for m in range(2):
        part = raw[:, 256 * m : 256 * m + 512]
        filtered.append(dot_t(part, strips[0]) + (dot_t(part, strips[1]) + dot_t(part, strips[2])))
    filtered = jnp.concatenate(filtered, axis=1)
    at_row = lax.broadcasted_iota(jnp.int32, (256, 512), 0) + 128
    at_col = lax.broadcasted_iota(jnp.int32, (256, 512), 1)
    band = jnp.where(jnp.abs(at_row - at_col) <= HALFRUN, 1.0, 0.0).astype(jnp.bfloat16)
    pieces = [jnp.concatenate([side, t, side], axis=1) for t in split_terms(jnp.abs(filtered))]
    summed = []
    for m in range(2):
        cut = [p[:, 256 * m : 256 * m + 512] for p in pieces]
        summed.append(dot_t(cut[0], band) + (dot_t(cut[1], band) + dot_t(cut[2], band)))
    summed = jnp.concatenate(summed, axis=1)
    at = lax.broadcasted_iota(jnp.int32, (1, SAMP), 1)
    counted = jnp.minimum(at + HALFRUN, SAMP - 1) - jnp.maximum(at - HALFRUN, 0) + 1
    envelope = summed / counted.astype(jnp.float32)
    whitened = filtered / (envelope + 1e-06)
    counts = jnp.broadcast_to(counts_ref[...].astype(jnp.float32), (128, channels)).T
    counts = jnp.concatenate([counts] * (SAMP // 128), axis=1)
    live = at.astype(jnp.float32) < counts
    whitened = jnp.where(live, whitened, 0.0)
    rounded = whitened.astype(jnp.bfloat16)
    out_ref[...] = rounded
    held = channels // BLK
    for number in range(NBLK):
        local = blocks_ref[number] - chan_ref[0] * held
        owned = jnp.logical_and(local >= 0, local < held)
        start = pl.multiple_of(jnp.clip(local, 0, held - 1) * BLK, BLK)
        rows = full_ref[pl.ds(start, BLK), :].astype(jnp.float32)
        rows = jnp.where(owned, rows, 0.0)
        contrib_ref[number * BLK : (number + 1) * BLK, :] = rows.astype(jnp.bfloat16)


def prep(raw, fir_taps, source_blocks, counts, chan):
    channels = raw.shape[0]
    smem = pl.BlockSpec(memory_space=pltpu.SMEM)
    vmem = pl.BlockSpec(memory_space=pltpu.VMEM)
    return pl.pallas_call(
        prep_body,
        in_specs=[smem, smem, vmem, vmem, vmem],
        out_specs=[vmem, vmem],
        out_shape=[
            jax.ShapeDtypeStruct((channels, SAMP), jnp.bfloat16),
            jax.ShapeDtypeStruct((NBLK * BLK, SAMP), jnp.bfloat16),
        ],
        scratch_shapes=[pltpu.VMEM((1, 512), jnp.float32)],
        name="prep",
    )(source_blocks, chan, raw, fir_taps.reshape(1, TAPS), counts)


def fill_lagged(rows, first, lagged_ref):
    span = SAMP + 128
    around = jnp.concatenate([rows, jnp.zeros((SRC_PAIR, 128), jnp.float32)], axis=1)
    shift = 128 - MAXLAG
    around = pltpu.roll(around, shift % 8, 1)
    for at in range(SRC_PAIR // 2):
        row = jnp.broadcast_to(around[first + at : first + at + 1, :], (128, span))
        rolled = pltpu.roll(row, shift - shift % 8, 1, stride=1, stride_axis=0)
        rolled = rolled.astype(jnp.bfloat16)
        lagged_ref[at * LAGPAD : at * LAGPAD + 128, :] = rolled[:, 128:]
        lagged_ref[at * LAGPAD + 128 : (at + 1) * LAGPAD, :] = rolled[: LAGPAD - 128, :SAMP]


def correlate_body(has_prev, is_last, *refs):
    refs = list(refs)
    core_ref, src_ref, recv_ref = refs[:3]
    refs = refs[3:]
    prev_ref = refs.pop(0) if has_prev else None
    if is_last:
        mine_ref, other_ref, acc_ref, first_ref, second_ref = refs
    else:
        acc_ref, first_ref, second_ref = refs
    window = pl.program_id(0)

    @pl.when(window == 0)
    def _():
        acc_ref[...] = prev_ref[...] if has_prev else jnp.zeros(acc_ref.shape, jnp.float32)

    rows = src_ref[0].astype(jnp.float32)
    receivers = recv_ref[0]
    half = SRC_PAIR // 2
    for number, lagged_ref in enumerate((first_ref, second_ref)):
        fill_lagged(rows, number * half, lagged_ref)
        got = dot_t(lagged_ref[...], receivers).reshape(half, LAGPAD, receivers.shape[0])
        acc_ref[number * half : (number + 1) * half] += got

    if is_last:

        @pl.when(window == pl.num_programs(0) - 1)
        def _():
            core = core_ref[0]
            mine_ref[...] = acc_ref[pl.ds(core * half, half), :NLAG, :]
            other_ref[...] = acc_ref[pl.ds((1 - core) * half, half), :NLAG, :]


def correlate(sources, receivers, off_x, base, prev, core, is_last):
    windows, local_width = receivers.shape[0], receivers.shape[1]
    acc_shape = (SRC_PAIR, LAGPAD, local_width)
    whole = lambda shape: pl.BlockSpec(shape, lambda w, core: (0,) * len(shape))
    half_shape = (SRC_PAIR // 2, NLAG, local_width)
    in_specs = [
        pl.BlockSpec((1, SRC_PAIR, SAMP), lambda w, core: (4 * (base + w) + off_x, 0, 0)),
        pl.BlockSpec((1, local_width, SAMP), lambda w, core: (w, 0, 0)),
    ]
    operands = [sources, receivers]
    if prev is not None:
        in_specs.append(whole(acc_shape))
        operands.append(prev)
    scratch = [pltpu.VMEM((SRC_PAIR // 2 * LAGPAD, SAMP), jnp.bfloat16)] * 2
    if is_last:
        out_specs = [whole(half_shape)] * 2
        out_shape = [jax.ShapeDtypeStruct(half_shape, jnp.float32)] * 2
        scratch = [pltpu.VMEM(acc_shape, jnp.float32)] + scratch
    else:
        out_specs = whole(acc_shape)
        out_shape = jax.ShapeDtypeStruct(acc_shape, jnp.float32)

    def body(*refs):
        correlate_body(prev is not None, is_last, *refs)

    return pl.pallas_call(
        body,
        grid_spec=pltpu.PrefetchScalarGridSpec(
            num_scalar_prefetch=1,
            grid=(windows,),
            in_specs=in_specs,
            out_specs=out_specs,
            scratch_shapes=scratch,
        ),
        out_shape=out_shape,
        name="correlate",
    )(core, *operands)


def deal_body(at_ref, *refs):
    at = at_ref[0]
    in_refs, out_refs = refs[:-4], refs[-4:]
    for by, out_ref in enumerate(out_refs):
        picked = (at + by) & 3
        if len(in_refs) == 2:
            both = [ref[picked].astype(jnp.float32) for ref in in_refs]
            out_ref[...] = (both[0] + both[1]).astype(jnp.bfloat16)
        else:
            for number, ref in enumerate(in_refs):
                out_ref[number] = ref[picked]


def deal(at, arrays):
    smem = pl.BlockSpec(memory_space=pltpu.SMEM)
    vmem = pl.BlockSpec(memory_space=pltpu.VMEM)
    return pl.pallas_call(
        deal_body,
        in_specs=[smem] + [vmem] * len(arrays),
        out_specs=[vmem] * 4,
        out_shape=[jax.ShapeDtypeStruct((4, SRC_PAIR, SAMP), jnp.bfloat16)] * 4,
        name="deal",
    )(at, *arrays)


def shifted(value, axis, by):
    size = lax.axis_size(axis)
    return lax.ppermute(value, axis, [(i, (i + by) % size) for i in range(size)])


def along_z(own):
    below, above = shifted(own, "z_hi", 1), shifted(own, "z_hi", -1)
    half = own.shape[0] // 2
    low = shifted(below[:half], "z_hi", 1)
    high = shifted(above[half:], "z_hi", -1)
    return jnp.stack([own, below, above, jnp.concatenate([low, high], axis=0)])


def shards(raw_traces, fir_taps, source_blocks, valid_counts):
    chan = lax.axis_index("chan").astype(jnp.int32)
    core = lax.axis_index("core").astype(jnp.int32).reshape(1)
    at_x = lax.axis_index("x").astype(jnp.int32)
    at_z = lax.axis_index("z_hi").astype(jnp.int32)
    chans, size_x, size_z = lax.axis_size("chan"), lax.axis_size("x"), lax.axis_size("z_hi")
    own, mine = prep(raw_traces[0], fir_taps, source_blocks, valid_counts, chan.reshape(1))
    bundle = along_z(own)
    step = 1
    while step < chans // 2:
        mine = mine + lax.ppermute(mine, "chan", [(i, i ^ step) for i in range(chans)])
        step *= 2
    theirs = lax.ppermute(mine, "chan", [(i, i ^ step) for i in range(chans)])
    mine, theirs, bundle = lax.optimization_barrier((mine, theirs, bundle))
    before, after = shifted(bundle, "x", 1), shifted(bundle, "x", -1)
    grouped = (size_x, size_z, SRC_PAIR, SAMP)
    parts = [v.reshape(grouped) for v in (mine, theirs)]
    dealt = deal(at_x.reshape(1), parts)
    dealt = [dealt[0]] + [shifted(dealt[by], "x", by) for by in range(1, 4)]
    dealt = deal(at_z.reshape(1), dealt)
    dealt = [dealt[0]] + [shifted(dealt[by], "z_hi", by) for by in range(1, 4)]
    sources = jnp.concatenate([dealt[0], dealt[1], dealt[3], dealt[2]], axis=0)
    total = correlate(sources, bundle, 0, 0, None, core, False)
    total, before, after = lax.optimization_barrier((total, before, after))
    half = bundle.shape[0] // 2
    low, high = shifted(before[:half], "x", 1), shifted(after[half:], "x", -1)
    total = correlate(sources, before, 1, 0, total, core, False)
    total = correlate(sources, after, 3, 0, total, core, False)
    total = correlate(sources, low, 2, 0, total, core, False)
    total = correlate(sources, high, 2, half, total, core, True)
    kept, passed = total
    got = shifted(passed, "core", 1)
    factor = 1.0 / math.sqrt(SAMP * size_x * size_z * 2)
    return (kept + got) * factor


def solution(mesh):
    chans, wins = mesh.devices.shape
    finer = Mesh(
        mesh.devices.reshape(chans, 4, wins // 8, 2), ("chan", "x", "z_hi", "core")
    )
    win = ("x", "z_hi", "core")
    return jax.shard_map(
        shards,
        mesh=finer,
        in_specs=(P(win, "chan", None), P(), P(), P(win, "chan")),
        out_specs=P(win, None, "chan"),
        check_vma=False,
    )
```

```python
import math

import jax
import jax.numpy as jnp
from jax import lax
from jax.experimental import pallas as pl
from jax.experimental.pallas import tpu as pltpu
from jax.sharding import Mesh, PartitionSpec as P

BLK = 64
NBLK = 2
SAMP = 512
TAPS = 65
HALFTAPS = 32
HALFRUN = 64
MAXLAG = 100
NLAG = 2 * MAXLAG + 1
LAGPAD = 208
SRC_PAIR = 8
PAIR = 2


def split_terms(x):
    hi = x.astype(jnp.bfloat16)
    rest = x - hi.astype(jnp.float32)
    mid = rest.astype(jnp.bfloat16)
    lo = (rest - mid.astype(jnp.float32)).astype(jnp.bfloat16)
    return hi, mid, lo


def dot_t(a, b):
    return lax.dot_general(a, b, (((1,), (1,)), ((), ())), preferred_element_type=jnp.float32)


def prep_body(blocks_ref, chan_ref, raw_ref, taps_ref, counts_ref, *refs):
    out_ref, contrib_ref, padded_ref = refs
    full_ref = out_ref
    channels = raw_ref.shape[0]
    side = jnp.zeros((channels, 128), jnp.bfloat16)
    raw = jnp.concatenate([side, raw_ref[...], side], axis=1)
    padded_ref[...] = jnp.zeros(padded_ref.shape, jnp.float32)
    padded_ref[:, :TAPS] = taps_ref[...]
    rows = jnp.broadcast_to(padded_ref[...], (256, 512))
    strips = split_terms(pltpu.roll(rows, 128 - HALFTAPS, 1, stride=1, stride_axis=0))
    filtered = []
    for m in range(2):
        part = raw[:, 256 * m : 256 * m + 512]
        filtered.append(dot_t(part, strips[0]) + (dot_t(part, strips[1]) + dot_t(part, strips[2])))
    filtered = jnp.concatenate(filtered, axis=1)
    at_row = lax.broadcasted_iota(jnp.int32, (256, 512), 0) + 128
    at_col = lax.broadcasted_iota(jnp.int32, (256, 512), 1)
    band = jnp.where(jnp.abs(at_row - at_col) <= HALFRUN, 1.0, 0.0).astype(jnp.bfloat16)
    pieces = [jnp.concatenate([side, t, side], axis=1) for t in split_terms(jnp.abs(filtered))]
    summed = []
    for m in range(2):
        cut = [p[:, 256 * m : 256 * m + 512] for p in pieces]
        summed.append(dot_t(cut[0], band) + (dot_t(cut[1], band) + dot_t(cut[2], band)))
    summed = jnp.concatenate(summed, axis=1)
    at = lax.broadcasted_iota(jnp.int32, (1, SAMP), 1)
    counted = jnp.minimum(at + HALFRUN, SAMP - 1) - jnp.maximum(at - HALFRUN, 0) + 1
    envelope = summed / counted.astype(jnp.float32)
    whitened = filtered / (envelope + 1e-06)
    counts = jnp.broadcast_to(counts_ref[...].astype(jnp.float32), (128, channels)).T
    counts = jnp.concatenate([counts] * (SAMP // 128), axis=1)
    live = at.astype(jnp.float32) < counts
    whitened = jnp.where(live, whitened, 0.0)
    rounded = whitened.astype(jnp.bfloat16)
    out_ref[...] = rounded
    held = channels // BLK
    for number in range(NBLK):
        local = blocks_ref[number] - chan_ref[0] * held
        owned = jnp.logical_and(local >= 0, local < held)
        start = pl.multiple_of(jnp.clip(local, 0, held - 1) * BLK, BLK)
        rows = full_ref[pl.ds(start, BLK), :].astype(jnp.float32)
        rows = jnp.where(owned, rows, 0.0)
        contrib_ref[number * BLK : (number + 1) * BLK, :] = rows.astype(jnp.bfloat16)


def prep(raw, fir_taps, source_blocks, counts, chan):
    channels = raw.shape[0]
    smem = pl.BlockSpec(memory_space=pltpu.SMEM)
    vmem = pl.BlockSpec(memory_space=pltpu.VMEM)
    return pl.pallas_call(
        prep_body,
        in_specs=[smem, smem, vmem, vmem, vmem],
        out_specs=[vmem, vmem],
        out_shape=[
            jax.ShapeDtypeStruct((channels, SAMP), jnp.bfloat16),
            jax.ShapeDtypeStruct((NBLK * BLK, SAMP), jnp.bfloat16),
        ],
        scratch_shapes=[pltpu.VMEM((1, 512), jnp.float32)],
        name="prep",
    )(source_blocks, chan, raw, fir_taps.reshape(1, TAPS), counts)


def fill_lagged(rows, first, lagged_ref):
    span = SAMP + 128
    around = jnp.concatenate([rows, jnp.zeros((SRC_PAIR, 128), jnp.float32)], axis=1)
    shift = 128 - MAXLAG
    around = pltpu.roll(around, shift % 8, 1)
    for at in range(SRC_PAIR // 2):
        row = jnp.broadcast_to(around[first + at : first + at + 1, :], (128, span))
        rolled = pltpu.roll(row, shift - shift % 8, 1, stride=1, stride_axis=0)
        rolled = rolled.astype(jnp.bfloat16)
        lagged_ref[at * LAGPAD : at * LAGPAD + 128, :] = rolled[:, 128:]
        lagged_ref[at * LAGPAD + 128 : (at + 1) * LAGPAD, :] = rolled[: LAGPAD - 128, :SAMP]


def correlate_body(has_prev, is_last, *refs):
    refs = list(refs)
    core_ref, src_ref, early_ref, late_ref = refs[:4]
    refs = refs[4:]
    prev_ref = refs.pop(0) if has_prev else None
    if is_last:
        mine_ref, other_ref, acc_ref, first_ref, second_ref = refs
    else:
        acc_ref, first_ref, second_ref = refs
    window = pl.program_id(0)

    @pl.when(window == 0)
    def _():
        acc_ref[...] = prev_ref[...] if has_prev else jnp.zeros(acc_ref.shape, jnp.float32)

    rows = src_ref[0].astype(jnp.float32)
    receivers = jnp.where(window < PAIR, early_ref[0], late_ref[0])
    half = SRC_PAIR // 2
    for number, lagged_ref in enumerate((first_ref, second_ref)):
        fill_lagged(rows, number * half, lagged_ref)
        got = dot_t(lagged_ref[...], receivers).reshape(half, LAGPAD, receivers.shape[0])
        acc_ref[number * half : (number + 1) * half] += got

    if is_last:

        @pl.when(window == pl.num_programs(0) - 1)
        def _():
            core = core_ref[0]
            mine_ref[...] = acc_ref[pl.ds(core * half, half), :NLAG, :]
            other_ref[...] = acc_ref[pl.ds((1 - core) * half, half), :NLAG, :]


def correlate(sources, early, late, prev, core, is_last):
    (early_x, early_z, early), (late_x, late_z, late) = early, late
    local_width = early.shape[1]
    acc_shape = (SRC_PAIR, LAGPAD, local_width)
    whole = lambda shape: pl.BlockSpec(shape, lambda w, core: (0,) * len(shape))
    half_shape = (SRC_PAIR // 2, NLAG, local_width)

    def source_at(w, core):
        at_early, at_late = 4 * (early_z + w) + early_x, 4 * (late_z + w - PAIR) + late_x
        return jnp.where(w < PAIR, at_early, at_late), 0, 0

    in_specs = [
        pl.BlockSpec((1, SRC_PAIR, SAMP), source_at),
        pl.BlockSpec((1, local_width, SAMP), lambda w, core: (jnp.minimum(w, PAIR - 1), 0, 0)),
        pl.BlockSpec((1, local_width, SAMP), lambda w, core: (jnp.maximum(w - PAIR, 0), 0, 0)),
    ]
    operands = [sources, early, late]
    if prev is not None:
        in_specs.append(whole(acc_shape))
        operands.append(prev)
    scratch = [pltpu.VMEM((SRC_PAIR // 2 * LAGPAD, SAMP), jnp.bfloat16)] * 2
    if is_last:
        out_specs = [whole(half_shape)] * 2
        out_shape = [jax.ShapeDtypeStruct(half_shape, jnp.float32)] * 2
        scratch = [pltpu.VMEM(acc_shape, jnp.float32)] + scratch
    else:
        out_specs = whole(acc_shape)
        out_shape = jax.ShapeDtypeStruct(acc_shape, jnp.float32)

    def body(*refs):
        correlate_body(prev is not None, is_last, *refs)

    return pl.pallas_call(
        body,
        grid_spec=pltpu.PrefetchScalarGridSpec(
            num_scalar_prefetch=1,
            grid=(2 * PAIR,),
            in_specs=in_specs,
            out_specs=out_specs,
            scratch_shapes=scratch,
        ),
        out_shape=out_shape,
        name="correlate",
    )(core, *operands)


def deal_body(at_ref, *refs):
    at = at_ref[0]
    in_refs, out_refs = refs[:-4], refs[-4:]
    for by, out_ref in enumerate(out_refs):
        picked = (at + by) & 3
        if len(in_refs) == 2:
            both = [ref[picked].astype(jnp.float32) for ref in in_refs]
            out_ref[...] = (both[0] + both[1]).astype(jnp.bfloat16)
        else:
            for number, ref in enumerate(in_refs):
                out_ref[number] = ref[picked]


def deal(at, arrays):
    smem = pl.BlockSpec(memory_space=pltpu.SMEM)
    vmem = pl.BlockSpec(memory_space=pltpu.VMEM)
    return pl.pallas_call(
        deal_body,
        in_specs=[smem] + [vmem] * len(arrays),
        out_specs=[vmem] * 4,
        out_shape=[jax.ShapeDtypeStruct((4, SRC_PAIR, SAMP), jnp.bfloat16)] * 4,
        name="deal",
    )(at, *arrays)


def shifted(value, axis, by):
    size = lax.axis_size(axis)
    return lax.ppermute(value, axis, [(i, (i + by) % size) for i in range(size)])


def shards(raw_traces, fir_taps, source_blocks, valid_counts):
    chan = lax.axis_index("chan").astype(jnp.int32)
    core = lax.axis_index("core").astype(jnp.int32).reshape(1)
    at_x = lax.axis_index("x").astype(jnp.int32)
    at_z = lax.axis_index("z_hi").astype(jnp.int32)
    chans, size_x, size_z = lax.axis_size("chan"), lax.axis_size("x"), lax.axis_size("z_hi")
    own, mine = prep(raw_traces[0], fir_taps, source_blocks, valid_counts, chan.reshape(1))
    below, above = shifted(own, "z_hi", 1), shifted(own, "z_hi", -1)
    half = own.shape[0] // 2
    opposite = [shifted(below[:half], "z_hi", 1), shifted(above[half:], "z_hi", -1)]

    def swap(value, step):
        return lax.ppermute(value, "chan", [(i, i ^ step) for i in range(chans)])

    step = chans // 2
    mine = mine + swap(mine, step)
    while step > 2:
        step //= 2
        mine = mine + swap(mine, step)
    grouped = (size_x, size_z, SRC_PAIR, SAMP)
    parts = [v.reshape(grouped) for v in (mine, swap(mine, step // 2))]
    dealt = deal(at_x.reshape(1), parts)
    dealt = [dealt[0]] + [shifted(dealt[by], "x", by) for by in range(1, 4)]
    low = jnp.stack([own, below])
    dealt, low = lax.optimization_barrier((dealt, low))
    before_low, after_low = shifted(low, "x", 1), shifted(low, "x", -1)
    high = jnp.stack([above, jnp.concatenate(opposite, axis=0)])
    dealt = deal(at_z.reshape(1), dealt)
    dealt = [dealt[0]] + [shifted(dealt[by], "z_hi", by) for by in range(1, 4)]
    dealt, high = lax.optimization_barrier((dealt, high))
    before_high, after_high = shifted(high, "x", 1), shifted(high, "x", -1)
    sources = jnp.concatenate([dealt[0], dealt[1], dealt[3], dealt[2]], axis=0)
    total = correlate(sources, (0, 0, low), (0, 2, high), None, core, False)
    total, before_low, after_low = lax.optimization_barrier((total, before_low, after_low))
    far_low = shifted(before_low, "x", 1)
    total = correlate(sources, (1, 0, before_low), (3, 0, after_low), total, core, False)
    total, before_high, after_high = lax.optimization_barrier((total, before_high, after_high))
    far_high = shifted(after_high, "x", -1)
    total = correlate(sources, (1, 2, before_high), (3, 2, after_high), total, core, False)
    total = correlate(sources, (2, 0, far_low), (2, 2, far_high), total, core, True)
    kept, passed = total
    got = shifted(passed, "core", 1)
    factor = 1.0 / math.sqrt(SAMP * size_x * size_z * 2)
    return (kept + got) * factor


def solution(mesh):
    chans, wins = mesh.devices.shape
    finer = Mesh(
        mesh.devices.reshape(chans, 4, wins // 8, 2), ("chan", "x", "z_hi", "core")
    )
    win = ("x", "z_hi", "core")
    return jax.shard_map(
        shards,
        mesh=finer,
        in_specs=(P(win, "chan", None), P(), P(), P(win, "chan")),
        out_specs=P(win, None, "chan"),
        check_vma=False,
    )
```

```python
import math

import jax
import jax.numpy as jnp
from jax import lax
from jax.experimental import pallas as pl
from jax.experimental.pallas import tpu as pltpu
from jax.sharding import Mesh, PartitionSpec as P

BLK = 64
NBLK = 2
SAMP = 512
TAPS = 65
HALFTAPS = 32
HALFRUN = 64
MAXLAG = 100
NLAG = 2 * MAXLAG + 1
LAGPAD = 208
SRC_PAIR = 8
PAIR = 2


def split_terms(x):
    hi = x.astype(jnp.bfloat16)
    rest = x - hi.astype(jnp.float32)
    mid = rest.astype(jnp.bfloat16)
    lo = (rest - mid.astype(jnp.float32)).astype(jnp.bfloat16)
    return hi, mid, lo


def dot_t(a, b):
    return lax.dot_general(a, b, (((1,), (1,)), ((), ())), preferred_element_type=jnp.float32)


def prep_body(blocks_ref, chan_ref, raw_ref, taps_ref, counts_ref, *refs):
    out_ref, contrib_ref, padded_ref = refs
    full_ref = out_ref
    channels = raw_ref.shape[0]
    side = jnp.zeros((channels, 128), jnp.bfloat16)
    raw = jnp.concatenate([side, raw_ref[...], side], axis=1)
    padded_ref[...] = jnp.zeros(padded_ref.shape, jnp.float32)
    padded_ref[:, :TAPS] = taps_ref[...]
    rows = jnp.broadcast_to(padded_ref[...], (256, 512))
    strips = split_terms(pltpu.roll(rows, 128 - HALFTAPS, 1, stride=1, stride_axis=0))
    filtered = []
    for m in range(2):
        part = raw[:, 256 * m : 256 * m + 512]
        filtered.append(dot_t(part, strips[0]) + (dot_t(part, strips[1]) + dot_t(part, strips[2])))
    filtered = jnp.concatenate(filtered, axis=1)
    at_row = lax.broadcasted_iota(jnp.int32, (256, 512), 0) + 128
    at_col = lax.broadcasted_iota(jnp.int32, (256, 512), 1)
    band = jnp.where(jnp.abs(at_row - at_col) <= HALFRUN, 1.0, 0.0).astype(jnp.bfloat16)
    pieces = [jnp.concatenate([side, t, side], axis=1) for t in split_terms(jnp.abs(filtered))]
    summed = []
    for m in range(2):
        cut = [p[:, 256 * m : 256 * m + 512] for p in pieces]
        summed.append(dot_t(cut[0], band) + (dot_t(cut[1], band) + dot_t(cut[2], band)))
    summed = jnp.concatenate(summed, axis=1)
    at = lax.broadcasted_iota(jnp.int32, (1, SAMP), 1)
    counted = jnp.minimum(at + HALFRUN, SAMP - 1) - jnp.maximum(at - HALFRUN, 0) + 1
    envelope = summed / counted.astype(jnp.float32)
    whitened = filtered / (envelope + 1e-06)
    counts = jnp.broadcast_to(counts_ref[...].astype(jnp.float32), (128, channels)).T
    counts = jnp.concatenate([counts] * (SAMP // 128), axis=1)
    live = at.astype(jnp.float32) < counts
    whitened = jnp.where(live, whitened, 0.0)
    rounded = whitened.astype(jnp.bfloat16)
    out_ref[...] = rounded
    held = channels // BLK
    for number in range(NBLK):
        local = blocks_ref[number] - chan_ref[0] * held
        owned = jnp.logical_and(local >= 0, local < held)
        start = pl.multiple_of(jnp.clip(local, 0, held - 1) * BLK, BLK)
        rows = full_ref[pl.ds(start, BLK), :].astype(jnp.float32)
        rows = jnp.where(owned, rows, 0.0)
        contrib_ref[number * BLK : (number + 1) * BLK, :] = rows.astype(jnp.bfloat16)


def prep(raw, fir_taps, source_blocks, counts, chan):
    channels = raw.shape[0]
    smem = pl.BlockSpec(memory_space=pltpu.SMEM)
    vmem = pl.BlockSpec(memory_space=pltpu.VMEM)
    return pl.pallas_call(
        prep_body,
        in_specs=[smem, smem, vmem, vmem, vmem],
        out_specs=[vmem, vmem],
        out_shape=[
            jax.ShapeDtypeStruct((channels, SAMP), jnp.bfloat16),
            jax.ShapeDtypeStruct((NBLK * BLK, SAMP), jnp.bfloat16),
        ],
        scratch_shapes=[pltpu.VMEM((1, 512), jnp.float32)],
        name="prep",
    )(source_blocks, chan, raw, fir_taps.reshape(1, TAPS), counts)


def fill_lagged(rows, first, lagged_ref):
    span = SAMP + 128
    around = jnp.concatenate([rows, jnp.zeros((SRC_PAIR, 128), jnp.float32)], axis=1)
    shift = 128 - MAXLAG
    around = pltpu.roll(around, shift % 8, 1)
    for at in range(SRC_PAIR // 2):
        row = jnp.broadcast_to(around[first + at : first + at + 1, :], (128, span))
        rolled = pltpu.roll(row, shift - shift % 8, 1, stride=1, stride_axis=0)
        rolled = rolled.astype(jnp.bfloat16)
        lagged_ref[at * LAGPAD : at * LAGPAD + 128, :] = rolled[:, 128:]
        lagged_ref[at * LAGPAD + 128 : (at + 1) * LAGPAD, :] = rolled[: LAGPAD - 128, :SAMP]


def correlate_body(has_prev, is_last, *refs):
    refs = list(refs)
    core_ref, src_ref, early_ref, late_ref = refs[:4]
    refs = refs[4:]
    prev_ref = refs.pop(0) if has_prev else None
    if is_last:
        mine_ref, other_ref, acc_ref, first_ref, second_ref = refs
    else:
        acc_ref, first_ref, second_ref = refs
    window = pl.program_id(0)

    @pl.when(window == 0)
    def _():
        acc_ref[...] = prev_ref[...] if has_prev else jnp.zeros(acc_ref.shape, jnp.float32)

    rows = src_ref[0].astype(jnp.float32)
    receivers = jnp.where(window < PAIR, early_ref[0], late_ref[0])
    half = SRC_PAIR // 2
    for number, lagged_ref in enumerate((first_ref, second_ref)):
        fill_lagged(rows, number * half, lagged_ref)
        got = dot_t(lagged_ref[...], receivers).reshape(half, LAGPAD, receivers.shape[0])
        acc_ref[number * half : (number + 1) * half] += got

    if is_last:

        @pl.when(window == pl.num_programs(0) - 1)
        def _():
            core = core_ref[0]
            for at in range(half):
                mine_ref[:, at, :] = acc_ref[core * half + at, :NLAG, :]
                other_ref[:, at, :] = acc_ref[(1 - core) * half + at, :NLAG, :]


def correlate(sources, early, late, prev, core, is_last):
    (early_x, early_z, early), (late_x, late_z, late) = early, late
    local_width = early.shape[1]
    acc_shape = (SRC_PAIR, LAGPAD, local_width)
    whole = lambda shape: pl.BlockSpec(shape, lambda w, core: (0,) * len(shape))
    half_shape = (NLAG, SRC_PAIR // 2, local_width)

    def source_at(w, core):
        at_early, at_late = 4 * (early_z + w) + early_x, 4 * (late_z + w - PAIR) + late_x
        return jnp.where(w < PAIR, at_early, at_late), 0, 0

    in_specs = [
        pl.BlockSpec((1, SRC_PAIR, SAMP), source_at),
        pl.BlockSpec((1, local_width, SAMP), lambda w, core: (jnp.minimum(w, PAIR - 1), 0, 0)),
        pl.BlockSpec((1, local_width, SAMP), lambda w, core: (jnp.maximum(w - PAIR, 0), 0, 0)),
    ]
    operands = [sources, early, late]
    if prev is not None:
        in_specs.append(whole(acc_shape))
        operands.append(prev)
    scratch = [pltpu.VMEM((SRC_PAIR // 2 * LAGPAD, SAMP), jnp.bfloat16)] * 2
    if is_last:
        out_specs = [whole(half_shape)] * 2
        out_shape = [jax.ShapeDtypeStruct(half_shape, jnp.float32)] * 2
        scratch = [pltpu.VMEM(acc_shape, jnp.float32)] + scratch
    else:
        out_specs = whole(acc_shape)
        out_shape = jax.ShapeDtypeStruct(acc_shape, jnp.float32)

    def body(*refs):
        correlate_body(prev is not None, is_last, *refs)

    return pl.pallas_call(
        body,
        grid_spec=pltpu.PrefetchScalarGridSpec(
            num_scalar_prefetch=1,
            grid=(2 * PAIR,),
            in_specs=in_specs,
            out_specs=out_specs,
            scratch_shapes=scratch,
        ),
        out_shape=out_shape,
        name="correlate",
    )(core, *operands)


def deal_body(at_ref, *refs):
    at = at_ref[0]
    in_refs, out_refs = refs[:-4], refs[-4:]
    for by, out_ref in enumerate(out_refs):
        picked = (at + by) & 3
        if len(in_refs) == 2:
            both = [ref[picked].astype(jnp.float32) for ref in in_refs]
            out_ref[...] = (both[0] + both[1]).astype(jnp.bfloat16)
        else:
            for number, ref in enumerate(in_refs):
                out_ref[number] = ref[picked]


def deal(at, arrays):
    smem = pl.BlockSpec(memory_space=pltpu.SMEM)
    vmem = pl.BlockSpec(memory_space=pltpu.VMEM)
    return pl.pallas_call(
        deal_body,
        in_specs=[smem] + [vmem] * len(arrays),
        out_specs=[vmem] * 4,
        out_shape=[jax.ShapeDtypeStruct((4, SRC_PAIR, SAMP), jnp.bfloat16)] * 4,
        name="deal",
    )(at, *arrays)


def shifted(value, axis, by):
    size = lax.axis_size(axis)
    return lax.ppermute(value, axis, [(i, (i + by) % size) for i in range(size)])


def shards(raw_traces, fir_taps, source_blocks, valid_counts):
    chan = lax.axis_index("chan").astype(jnp.int32)
    core = lax.axis_index("core").astype(jnp.int32).reshape(1)
    at_x = lax.axis_index("x").astype(jnp.int32)
    at_z = lax.axis_index("z_hi").astype(jnp.int32)
    chans, size_x, size_z = lax.axis_size("chan"), lax.axis_size("x"), lax.axis_size("z_hi")
    own, mine = prep(raw_traces[0], fir_taps, source_blocks, valid_counts, chan.reshape(1))
    below, above = shifted(own, "z_hi", 1), shifted(own, "z_hi", -1)

    def swap(value, step):
        return lax.ppermute(value, "chan", [(i, i ^ step) for i in range(chans)])

    step = chans // 2
    mine = mine + swap(mine, step)
    while step > 2:
        step //= 2
        mine = mine + swap(mine, step)
    grouped = (size_x, size_z, SRC_PAIR, SAMP)
    parts = [v.reshape(grouped) for v in (mine, swap(mine, step // 2))]
    dealt = deal(at_x.reshape(1), parts)
    dealt = [dealt[0]] + [shifted(dealt[by], "x", by) for by in range(1, 4)]
    dealt, below, above = lax.optimization_barrier((dealt, below, above))
    low = jnp.stack([own, below])
    before_low, after_low = shifted(low, "x", 1), shifted(low, "x", -1)
    half = own.shape[0] // 2
    opposite = [shifted(below[:half], "z_hi", 1), shifted(above[half:], "z_hi", -1)]
    high = jnp.stack([above, jnp.concatenate(opposite, axis=0)])
    dealt = deal(at_z.reshape(1), dealt)
    dealt = [dealt[0]] + [shifted(dealt[by], "z_hi", by) for by in range(1, 4)]
    dealt, high = lax.optimization_barrier((dealt, high))
    before_high, after_high = shifted(high, "x", 1), shifted(high, "x", -1)
    sources = jnp.concatenate([dealt[0], dealt[1], dealt[3], dealt[2]], axis=0)
    total = correlate(sources, (0, 0, low), (0, 2, high), None, core, False)
    total, before_low, after_low = lax.optimization_barrier((total, before_low, after_low))
    far_low = shifted(before_low, "x", 1)
    total = correlate(sources, (1, 0, before_low), (3, 0, after_low), total, core, False)
    total, before_high, after_high = lax.optimization_barrier((total, before_high, after_high))
    far_high = shifted(after_high, "x", -1)
    total = correlate(sources, (1, 2, before_high), (3, 2, after_high), total, core, False)
    total = correlate(sources, (2, 0, far_low), (2, 2, far_high), total, core, True)
    kept, passed = total
    got = shifted(passed, "core", 1)
    factor = 1.0 / math.sqrt(SAMP * size_x * size_z * 2)
    return jnp.transpose((kept + got) * factor, (1, 0, 2))


def solution(mesh):
    chans, wins = mesh.devices.shape
    finer = Mesh(
        mesh.devices.reshape(chans, 4, wins // 8, 2), ("chan", "x", "z_hi", "core")
    )
    win = ("x", "z_hi", "core")
    return jax.shard_map(
        shards,
        mesh=finer,
        in_specs=(P(win, "chan", None), P(), P(), P(win, "chan")),
        out_specs=P(win, None, "chan"),
        check_vma=False,
    )
```

```python
import math

import jax
import jax.numpy as jnp
from jax import lax
from jax.experimental import pallas as pl
from jax.experimental.pallas import tpu as pltpu
from jax.sharding import Mesh, PartitionSpec as P

BLK = 64
NBLK = 2
SAMP = 512
TAPS = 65
HALFTAPS = 32
HALFRUN = 64
MAXLAG = 100
NLAG = 2 * MAXLAG + 1
LAGPAD = 208
SRC_PAIR = 8
PAIR = 2


def split_terms(x):
    hi = x.astype(jnp.bfloat16)
    rest = x - hi.astype(jnp.float32)
    mid = rest.astype(jnp.bfloat16)
    lo = (rest - mid.astype(jnp.float32)).astype(jnp.bfloat16)
    return hi, mid, lo


def dot_t(a, b):
    return lax.dot_general(a, b, (((1,), (1,)), ((), ())), preferred_element_type=jnp.float32)


def prep_body(blocks_ref, chan_ref, raw_ref, taps_ref, counts_ref, *refs):
    out_ref, contrib_ref, padded_ref = refs
    full_ref = out_ref
    channels = raw_ref.shape[0]
    side = jnp.zeros((channels, 128), jnp.bfloat16)
    raw = jnp.concatenate([side, raw_ref[...], side], axis=1)
    padded_ref[...] = jnp.zeros(padded_ref.shape, jnp.float32)
    padded_ref[:, :TAPS] = taps_ref[...]
    rows = jnp.broadcast_to(padded_ref[...], (256, 512))
    strips = split_terms(pltpu.roll(rows, 128 - HALFTAPS, 1, stride=1, stride_axis=0))
    filtered = []
    for m in range(2):
        part = raw[:, 256 * m : 256 * m + 512]
        filtered.append(dot_t(part, strips[0]) + (dot_t(part, strips[1]) + dot_t(part, strips[2])))
    filtered = jnp.concatenate(filtered, axis=1)
    at_row = lax.broadcasted_iota(jnp.int32, (256, 512), 0) + 128
    at_col = lax.broadcasted_iota(jnp.int32, (256, 512), 1)
    band = jnp.where(jnp.abs(at_row - at_col) <= HALFRUN, 1.0, 0.0).astype(jnp.bfloat16)
    pieces = [jnp.concatenate([side, t, side], axis=1) for t in split_terms(jnp.abs(filtered))]
    summed = []
    for m in range(2):
        cut = [p[:, 256 * m : 256 * m + 512] for p in pieces]
        summed.append(dot_t(cut[0], band) + (dot_t(cut[1], band) + dot_t(cut[2], band)))
    summed = jnp.concatenate(summed, axis=1)
    at = lax.broadcasted_iota(jnp.int32, (1, SAMP), 1)
    counted = jnp.minimum(at + HALFRUN, SAMP - 1) - jnp.maximum(at - HALFRUN, 0) + 1
    envelope = summed / counted.astype(jnp.float32)
    whitened = filtered / (envelope + 1e-06)
    counts = jnp.broadcast_to(counts_ref[...].astype(jnp.float32), (128, channels)).T
    counts = jnp.concatenate([counts] * (SAMP // 128), axis=1)
    live = at.astype(jnp.float32) < counts
    whitened = jnp.where(live, whitened, 0.0)
    rounded = whitened.astype(jnp.bfloat16)
    out_ref[...] = rounded
    held = channels // BLK
    for number in range(NBLK):
        local = blocks_ref[number] - chan_ref[0] * held
        owned = jnp.logical_and(local >= 0, local < held)
        start = pl.multiple_of(jnp.clip(local, 0, held - 1) * BLK, BLK)
        rows = full_ref[pl.ds(start, BLK), :].astype(jnp.float32)
        rows = jnp.where(owned, rows, 0.0)
        contrib_ref[number * BLK : (number + 1) * BLK, :] = rows.astype(jnp.bfloat16)


def prep(raw, fir_taps, source_blocks, counts, chan):
    channels = raw.shape[0]
    smem = pl.BlockSpec(memory_space=pltpu.SMEM)
    vmem = pl.BlockSpec(memory_space=pltpu.VMEM)
    return pl.pallas_call(
        prep_body,
        in_specs=[smem, smem, vmem, vmem, vmem],
        out_specs=[vmem, vmem],
        out_shape=[
            jax.ShapeDtypeStruct((channels, SAMP), jnp.bfloat16),
            jax.ShapeDtypeStruct((NBLK * BLK, SAMP), jnp.bfloat16),
        ],
        scratch_shapes=[pltpu.VMEM((1, 512), jnp.float32)],
        name="prep",
    )(source_blocks, chan, raw, fir_taps.reshape(1, TAPS), counts)


def fill_lagged(rows, first, lagged_ref):
    span = SAMP + 128
    around = jnp.concatenate([rows, jnp.zeros((SRC_PAIR, 128), jnp.float32)], axis=1)
    shift = 128 - MAXLAG
    around = pltpu.roll(around, shift % 8, 1)
    for at in range(SRC_PAIR // 2):
        row = jnp.broadcast_to(around[first + at : first + at + 1, :], (128, span))
        rolled = pltpu.roll(row, shift - shift % 8, 1, stride=1, stride_axis=0)
        rolled = rolled.astype(jnp.bfloat16)
        lagged_ref[at * LAGPAD : at * LAGPAD + 128, :] = rolled[:, 128:]
        lagged_ref[at * LAGPAD + 128 : (at + 1) * LAGPAD, :] = rolled[: LAGPAD - 128, :SAMP]


def correlate_body(pieces, has_prev, is_last, *refs):
    refs = list(refs)
    core_ref, src_ref = refs[:2]
    recv_refs, refs = refs[2 : 2 + pieces], refs[2 + pieces :]
    prev_ref = refs.pop(0) if has_prev else None
    if is_last:
        mine_ref, other_ref, acc_ref, first_ref, second_ref = refs
    else:
        acc_ref, first_ref, second_ref = refs
    window = pl.program_id(0)

    @pl.when(window == 0)
    def _():
        acc_ref[...] = prev_ref[...] if has_prev else jnp.zeros(acc_ref.shape, jnp.float32)

    rows = src_ref[0].astype(jnp.float32)
    receivers = recv_refs[-1][0]
    for number in reversed(range(pieces - 1)):
        receivers = jnp.where(window < PAIR * (number + 1), recv_refs[number][0], receivers)
    half = SRC_PAIR // 2
    for number, lagged_ref in enumerate((first_ref, second_ref)):
        fill_lagged(rows, number * half, lagged_ref)
        got = dot_t(lagged_ref[...], receivers).reshape(half, LAGPAD, receivers.shape[0])
        acc_ref[number * half : (number + 1) * half] += got

    if is_last:

        @pl.when(window == pl.num_programs(0) - 1)
        def _():
            core = core_ref[0]
            for at in range(half):
                mine_ref[:, at, :] = acc_ref[core * half + at, :NLAG, :]
                other_ref[:, at, :] = acc_ref[(1 - core) * half + at, :NLAG, :]


def correlate(sources, pieces, prev, core, is_last):
    local_width = pieces[0][2].shape[1]
    acc_shape = (SRC_PAIR, LAGPAD, local_width)
    whole = lambda shape: pl.BlockSpec(shape, lambda w, core: (0,) * len(shape))
    half_shape = (NLAG, SRC_PAIR // 2, local_width)

    def source_at(w, core):
        at = 0
        for number, (x_back, z_at, _) in reversed(list(enumerate(pieces))):
            here = 4 * (z_at + w - PAIR * number) + x_back
            at = jnp.where(w < PAIR * (number + 1), here, at)
        return at, 0, 0

    def piece_at(number):
        return lambda w, core: (jnp.clip(w - PAIR * number, 0, PAIR - 1), 0, 0)

    in_specs = [pl.BlockSpec((1, SRC_PAIR, SAMP), source_at)]
    for number in range(len(pieces)):
        in_specs.append(pl.BlockSpec((1, local_width, SAMP), piece_at(number)))
    operands = [sources] + [piece for _, _, piece in pieces]
    if prev is not None:
        in_specs.append(whole(acc_shape))
        operands.append(prev)
    scratch = [pltpu.VMEM((SRC_PAIR // 2 * LAGPAD, SAMP), jnp.bfloat16)] * 2
    if is_last:
        out_specs = [whole(half_shape)] * 2
        out_shape = [jax.ShapeDtypeStruct(half_shape, jnp.float32)] * 2
        scratch = [pltpu.VMEM(acc_shape, jnp.float32)] + scratch
    else:
        out_specs = whole(acc_shape)
        out_shape = jax.ShapeDtypeStruct(acc_shape, jnp.float32)

    def body(*refs):
        correlate_body(len(pieces), prev is not None, is_last, *refs)

    return pl.pallas_call(
        body,
        grid_spec=pltpu.PrefetchScalarGridSpec(
            num_scalar_prefetch=1,
            grid=(len(pieces) * PAIR,),
            in_specs=in_specs,
            out_specs=out_specs,
            scratch_shapes=scratch,
        ),
        out_shape=out_shape,
        name="correlate",
    )(core, *operands)


def deal_body(at_ref, *refs):
    at = at_ref[0]
    in_refs, out_refs = refs[:-4], refs[-4:]
    for by, out_ref in enumerate(out_refs):
        picked = (at + by) & 3
        if len(in_refs) == 2:
            both = [ref[picked].astype(jnp.float32) for ref in in_refs]
            out_ref[...] = (both[0] + both[1]).astype(jnp.bfloat16)
        else:
            for number, ref in enumerate(in_refs):
                out_ref[number] = ref[picked]


def deal(at, arrays):
    smem = pl.BlockSpec(memory_space=pltpu.SMEM)
    vmem = pl.BlockSpec(memory_space=pltpu.VMEM)
    return pl.pallas_call(
        deal_body,
        in_specs=[smem] + [vmem] * len(arrays),
        out_specs=[vmem] * 4,
        out_shape=[jax.ShapeDtypeStruct((4, SRC_PAIR, SAMP), jnp.bfloat16)] * 4,
        name="deal",
    )(at, *arrays)


def shifted(value, axis, by):
    size = lax.axis_size(axis)
    return lax.ppermute(value, axis, [(i, (i + by) % size) for i in range(size)])


def shards(raw_traces, fir_taps, source_blocks, valid_counts):
    chan = lax.axis_index("chan").astype(jnp.int32)
    core = lax.axis_index("core").astype(jnp.int32).reshape(1)
    at_x = lax.axis_index("x").astype(jnp.int32)
    at_z = lax.axis_index("z_hi").astype(jnp.int32)
    chans, size_x, size_z = lax.axis_size("chan"), lax.axis_size("x"), lax.axis_size("z_hi")
    own, mine = prep(raw_traces[0], fir_taps, source_blocks, valid_counts, chan.reshape(1))
    below, above = shifted(own, "z_hi", 1), shifted(own, "z_hi", -1)

    def swap(value, step):
        return lax.ppermute(value, "chan", [(i, i ^ step) for i in range(chans)])

    step = chans // 2
    mine = mine + swap(mine, step)
    while step > 2:
        step //= 2
        mine = mine + swap(mine, step)
    grouped = (size_x, size_z, SRC_PAIR, SAMP)
    parts = [v.reshape(grouped) for v in (mine, swap(mine, step // 2))]
    dealt = deal(at_x.reshape(1), parts)
    dealt = [dealt[0]] + [shifted(dealt[by], "x", by) for by in range(1, 4)]
    dealt, below, above = lax.optimization_barrier((dealt, below, above))
    low = jnp.stack([own, below])
    before_low, after_low = shifted(low, "x", 1), shifted(low, "x", -1)
    half = own.shape[0] // 2
    opposite = [shifted(below[:half], "z_hi", 1), shifted(above[half:], "z_hi", -1)]
    high = jnp.stack([above, jnp.concatenate(opposite, axis=0)])
    dealt = deal(at_z.reshape(1), dealt)
    dealt = [dealt[0]] + [shifted(dealt[by], "z_hi", by) for by in range(1, 4)]
    dealt, high = lax.optimization_barrier((dealt, high))
    before_high, after_high = shifted(high, "x", 1), shifted(high, "x", -1)
    sources = jnp.concatenate([dealt[0], dealt[1], dealt[3], dealt[2]], axis=0)
    sources, before_low, after_low = lax.optimization_barrier((sources, before_low, after_low))
    far_low = shifted(before_low, "x", 1)
    near = [(0, 0, low), (0, 2, high), (1, 0, before_low), (3, 0, after_low)]
    total = correlate(sources, near, None, core, False)
    total, before_high, after_high = lax.optimization_barrier((total, before_high, after_high))
    far_high = shifted(after_high, "x", -1)
    total = correlate(sources, [(1, 2, before_high), (3, 2, after_high)], total, core, False)
    total = correlate(sources, [(2, 0, far_low), (2, 2, far_high)], total, core, True)
    kept, passed = total
    got = shifted(passed, "core", 1)
    factor = 1.0 / math.sqrt(SAMP * size_x * size_z * 2)
    return jnp.transpose((kept + got) * factor, (1, 0, 2))


def solution(mesh):
    chans, wins = mesh.devices.shape
    finer = Mesh(
        mesh.devices.reshape(chans, 4, wins // 8, 2), ("chan", "x", "z_hi", "core")
    )
    win = ("x", "z_hi", "core")
    return jax.shard_map(
        shards,
        mesh=finer,
        in_specs=(P(win, "chan", None), P(), P(), P(win, "chan")),
        out_specs=P(win, None, "chan"),
        check_vma=False,
    )
```

```python
import math

import jax
import jax.numpy as jnp
from jax import lax
from jax.experimental import pallas as pl
from jax.experimental.pallas import tpu as pltpu
from jax.sharding import Mesh, PartitionSpec as P

BLK = 64
NBLK = 2
SAMP = 512
TAPS = 65
HALFTAPS = 32
HALFRUN = 64
MAXLAG = 100
NLAG = 2 * MAXLAG + 1
LAGPAD = 208
SRC_PAIR = 8
PAIR = 2


def split_terms(x):
    hi = x.astype(jnp.bfloat16)
    rest = x - hi.astype(jnp.float32)
    mid = rest.astype(jnp.bfloat16)
    lo = (rest - mid.astype(jnp.float32)).astype(jnp.bfloat16)
    return hi, mid, lo


def dot_t(a, b):
    return lax.dot_general(a, b, (((1,), (1,)), ((), ())), preferred_element_type=jnp.float32)


def prep_body(blocks_ref, chan_ref, raw_ref, taps_ref, counts_ref, *refs):
    out_ref, contrib_ref, padded_ref = refs
    full_ref = out_ref
    channels = raw_ref.shape[0]
    side = jnp.zeros((channels, 128), jnp.bfloat16)
    raw = jnp.concatenate([side, raw_ref[...], side], axis=1)
    padded_ref[...] = jnp.zeros(padded_ref.shape, jnp.float32)
    padded_ref[:, :TAPS] = taps_ref[...]
    rows = jnp.broadcast_to(padded_ref[...], (256, 512))
    strips = split_terms(pltpu.roll(rows, 128 - HALFTAPS, 1, stride=1, stride_axis=0))
    filtered = []
    for m in range(2):
        part = raw[:, 256 * m : 256 * m + 512]
        filtered.append(dot_t(part, strips[0]) + (dot_t(part, strips[1]) + dot_t(part, strips[2])))
    filtered = jnp.concatenate(filtered, axis=1)
    at_row = lax.broadcasted_iota(jnp.int32, (256, 512), 0) + 128
    at_col = lax.broadcasted_iota(jnp.int32, (256, 512), 1)
    band = jnp.where(jnp.abs(at_row - at_col) <= HALFRUN, 1.0, 0.0).astype(jnp.bfloat16)
    pieces = [jnp.concatenate([side, t, side], axis=1) for t in split_terms(jnp.abs(filtered))]
    summed = []
    for m in range(2):
        cut = [p[:, 256 * m : 256 * m + 512] for p in pieces]
        summed.append(dot_t(cut[0], band) + (dot_t(cut[1], band) + dot_t(cut[2], band)))
    summed = jnp.concatenate(summed, axis=1)
    at = lax.broadcasted_iota(jnp.int32, (1, SAMP), 1)
    counted = jnp.minimum(at + HALFRUN, SAMP - 1) - jnp.maximum(at - HALFRUN, 0) + 1
    envelope = summed / counted.astype(jnp.float32)
    whitened = filtered / (envelope + 1e-06)
    counts = jnp.broadcast_to(counts_ref[...].astype(jnp.float32), (128, channels)).T
    counts = jnp.concatenate([counts] * (SAMP // 128), axis=1)
    live = at.astype(jnp.float32) < counts
    whitened = jnp.where(live, whitened, 0.0)
    rounded = whitened.astype(jnp.bfloat16)
    out_ref[...] = rounded
    held = channels // BLK
    for number in range(NBLK):
        local = blocks_ref[number] - chan_ref[0] * held
        owned = jnp.logical_and(local >= 0, local < held)
        start = pl.multiple_of(jnp.clip(local, 0, held - 1) * BLK, BLK)
        rows = full_ref[pl.ds(start, BLK), :].astype(jnp.float32)
        rows = jnp.where(owned, rows, 0.0)
        contrib_ref[number * BLK : (number + 1) * BLK, :] = rows.astype(jnp.bfloat16)


def prep(raw, fir_taps, source_blocks, counts, chan):
    channels = raw.shape[0]
    smem = pl.BlockSpec(memory_space=pltpu.SMEM)
    vmem = pl.BlockSpec(memory_space=pltpu.VMEM)
    return pl.pallas_call(
        prep_body,
        in_specs=[smem, smem, vmem, vmem, vmem],
        out_specs=[vmem, vmem],
        out_shape=[
            jax.ShapeDtypeStruct((channels, SAMP), jnp.bfloat16),
            jax.ShapeDtypeStruct((NBLK * BLK, SAMP), jnp.bfloat16),
        ],
        scratch_shapes=[pltpu.VMEM((1, 512), jnp.float32)],
        name="prep",
    )(source_blocks, chan, raw, fir_taps.reshape(1, TAPS), counts)


def fill_lagged(rows, first, lagged_ref):
    span = SAMP + 128
    around = jnp.concatenate([rows, jnp.zeros((SRC_PAIR, 128), jnp.float32)], axis=1)
    shift = 128 - MAXLAG
    around = pltpu.roll(around, shift % 8, 1)
    for at in range(SRC_PAIR // 2):
        row = jnp.broadcast_to(around[first + at : first + at + 1, :], (128, span))
        rolled = pltpu.roll(row, shift - shift % 8, 1, stride=1, stride_axis=0)
        rolled = rolled.astype(jnp.bfloat16)
        lagged_ref[at * LAGPAD : at * LAGPAD + 128, :] = rolled[:, 128:]
        lagged_ref[at * LAGPAD + 128 : (at + 1) * LAGPAD, :] = rolled[: LAGPAD - 128, :SAMP]


def correlate_body(pieces, has_prev, is_last, *refs):
    refs = list(refs)
    _, core_ref, src_ref = refs[:3]
    recv_refs, refs = refs[3 : 3 + pieces], refs[3 + pieces :]
    prev_ref = refs.pop(0) if has_prev else None
    if is_last:
        mine_ref, other_ref, acc_ref, first_ref, second_ref = refs
    else:
        acc_ref, first_ref, second_ref = refs
    window = pl.program_id(0)

    @pl.when(window == 0)
    def _():
        acc_ref[...] = prev_ref[...] if has_prev else jnp.zeros(acc_ref.shape, jnp.float32)

    rows = src_ref[0].astype(jnp.float32)
    receivers = recv_refs[-1][0]
    for number in reversed(range(pieces - 1)):
        receivers = jnp.where(window < PAIR * (number + 1), recv_refs[number][0], receivers)
    half = SRC_PAIR // 2
    for number, lagged_ref in enumerate((first_ref, second_ref)):
        fill_lagged(rows, number * half, lagged_ref)
        got = dot_t(lagged_ref[...], receivers).reshape(half, LAGPAD, receivers.shape[0])
        acc_ref[number * half : (number + 1) * half] += got

    if is_last:

        @pl.when(window == pl.num_programs(0) - 1)
        def _():
            core = core_ref[0]
            for at in range(half):
                mine_ref[:, at, :] = acc_ref[core * half + at, :NLAG, :]
                other_ref[:, at, :] = acc_ref[(1 - core) * half + at, :NLAG, :]


def correlate(table, sources, pieces, prev, core, is_last):
    local_width = pieces[0][2].shape[1]
    acc_shape = (SRC_PAIR, LAGPAD, local_width)
    whole = lambda shape: pl.BlockSpec(shape, lambda w, table, core: (0,) * len(shape))
    half_shape = (NLAG, SRC_PAIR // 2, local_width)

    def source_at(w, table, core):
        at = 0
        for number, (x_back, z_at, _) in reversed(list(enumerate(pieces))):
            here = 4 * (z_at + w - PAIR * number) + x_back
            at = jnp.where(w < PAIR * (number + 1), here, at)
        return table[at], 0, 0

    def piece_at(number):
        return lambda w, table, core: (jnp.clip(w - PAIR * number, 0, PAIR - 1), 0, 0)

    in_specs = [pl.BlockSpec((1, SRC_PAIR, SAMP), source_at)]
    for number in range(len(pieces)):
        in_specs.append(pl.BlockSpec((1, local_width, SAMP), piece_at(number)))
    operands = [sources] + [piece for _, _, piece in pieces]
    if prev is not None:
        in_specs.append(whole(acc_shape))
        operands.append(prev)
    scratch = [pltpu.VMEM((SRC_PAIR // 2 * LAGPAD, SAMP), jnp.bfloat16)] * 2
    if is_last:
        out_specs = [whole(half_shape)] * 2
        out_shape = [jax.ShapeDtypeStruct(half_shape, jnp.float32)] * 2
        scratch = [pltpu.VMEM(acc_shape, jnp.float32)] + scratch
    else:
        out_specs = whole(acc_shape)
        out_shape = jax.ShapeDtypeStruct(acc_shape, jnp.float32)

    def body(*refs):
        correlate_body(len(pieces), prev is not None, is_last, *refs)

    return pl.pallas_call(
        body,
        grid_spec=pltpu.PrefetchScalarGridSpec(
            num_scalar_prefetch=2,
            grid=(len(pieces) * PAIR,),
            in_specs=in_specs,
            out_specs=out_specs,
            scratch_shapes=scratch,
        ),
        out_shape=out_shape,
        name="correlate",
    )(table, core, *operands)


def shifted(value, axis, by):
    size = lax.axis_size(axis)
    return lax.ppermute(value, axis, [(i, (i + by) % size) for i in range(size)])


def shards(raw_traces, fir_taps, source_blocks, valid_counts):
    chan = lax.axis_index("chan").astype(jnp.int32)
    core = lax.axis_index("core").astype(jnp.int32).reshape(1)
    at_x = lax.axis_index("x").astype(jnp.int32)
    at_z = lax.axis_index("z_hi").astype(jnp.int32)
    chans, size_x, size_z = lax.axis_size("chan"), lax.axis_size("x"), lax.axis_size("z_hi")
    own, mine = prep(raw_traces[0], fir_taps, source_blocks, valid_counts, chan.reshape(1))
    below, above = shifted(own, "z_hi", 1), shifted(own, "z_hi", -1)

    def swap(value, step):
        return lax.ppermute(value, "chan", [(i, i ^ step) for i in range(chans)])

    step = chans // 2
    mine = mine + swap(mine, step)
    while step > 2:
        step //= 2
        mine = mine + swap(mine, step)
    mine = mine + swap(mine, step // 2)
    mine = mine.reshape(size_x * size_z, SRC_PAIR, SAMP)
    sources = lax.all_to_all(mine, ("x", "z_hi"), split_axis=0, concat_axis=0, tiled=True)
    sources, below, above = lax.optimization_barrier((sources, below, above))
    places = jnp.arange(size_x * size_z, dtype=jnp.int32)
    z_at, x_back = places >> 2, places & 3
    z_off = jnp.where(z_at == 3, 2, jnp.where(z_at == 2, 1, -z_at))
    table = ((at_x - x_back) & (size_x - 1)) * size_z + ((at_z + z_off) & (size_z - 1))
    low = jnp.stack([own, below])
    before_low, after_low = shifted(low, "x", 1), shifted(low, "x", -1)
    half = own.shape[0] // 2
    opposite = [shifted(below[:half], "z_hi", 1), shifted(above[half:], "z_hi", -1)]
    high = jnp.stack([above, jnp.concatenate(opposite, axis=0)])
    before_high, after_high = shifted(high, "x", 1), shifted(high, "x", -1)
    sources, before_low, after_low = lax.optimization_barrier((sources, before_low, after_low))
    far_low = shifted(before_low, "x", 1)
    near = [(0, 0, low), (0, 2, high), (1, 0, before_low), (3, 0, after_low)]
    total = correlate(table, sources, near, None, core, False)
    total, before_high, after_high = lax.optimization_barrier((total, before_high, after_high))
    far_high = shifted(after_high, "x", -1)
    total = correlate(table, sources, [(1, 2, before_high), (3, 2, after_high)], total, core, False)
    total = correlate(table, sources, [(2, 0, far_low), (2, 2, far_high)], total, core, True)
    kept, passed = total
    got = shifted(passed, "core", 1)
    factor = 1.0 / math.sqrt(SAMP * size_x * size_z * 2)
    return jnp.transpose((kept + got) * factor, (1, 0, 2))


def solution(mesh):
    chans, wins = mesh.devices.shape
    finer = Mesh(
        mesh.devices.reshape(chans, 4, wins // 8, 2), ("chan", "x", "z_hi", "core")
    )
    win = ("x", "z_hi", "core")
    return jax.shard_map(
        shards,
        mesh=finer,
        in_specs=(P(win, "chan", None), P(), P(), P(win, "chan")),
        out_specs=P(win, None, "chan"),
        check_vma=False,
    )
```
